512 devices in a mesh: section: 16 (over x, z_lo), expert: 32 (over z_hi, y, core).
Axes of the slice: x: 4, y: 4, z: 16 (z_hi: 4, z_lo: 4; z = z_hi * 4 + z_lo), core: 2. Of those that a mesh axis runs over, the one named last changes fastest.
Arguments:
- tokens: bfloat16 [16, 512, 4096], P('section', 'expert'), may hold values from -6 to 6
- norm_gain: float32 [16, 4096], P('section'), may hold values from 0.1 to 1.9
- first_routes: int32 [16, 512, 1], P('section', 'expert'), may hold values from 0 to 3; in each aligned block of 16 rows (0 to 15, 16 to 31, ..., all dimensions but the last counted through in order) at most 5 rows name the same one
- first_gates: float32 [16, 512, 1], P('section', 'expert'), may hold values from 0.25 to 2
- second_routes: int32 [16, 512, 1], P('section', 'expert'), may hold values from 0 to 3; in each aligned block of 16 rows (0 to 15, 16 to 31, ..., all dimensions but the last counted through in order) at most 5 rows name the same one
- second_gates: float32 [16, 512, 1], P('section', 'expert'), may hold values from 0.25 to 2
- gate_proj: bfloat16 [16, 32, 4096, 128], P('section', 'expert'), may hold values from -0.09375 to 0.09375
- up_proj: bfloat16 [16, 32, 4096, 128], P('section', 'expert'), may hold values from -0.09375 to 0.09375
- down_proj: bfloat16 [16, 32, 128, 4096], P('section', 'expert'), may hold values from -0.1875 to 0.1875
Outputs:
- mixed: bfloat16 [16, 512, 4096], P('section', 'expert')
The draws below stay inside these ranges and needn't reach their ends.
Inputs may be any that keep to these rules, and one draw needn't show every extreme that they name: `first_routes`: within the 16 rows of one device, no expert id appears more than 5 times, and in some devices one id appears exactly 5 times. `second_routes`: within the 16 rows of one device, no expert id appears more than 5 times, and in some devices one id appears exactly 5 times.
All inputs are finite; a program needn't handle non-finite values.
Results may differ from the reference program's by a relative error of at most 0.0078.
Values may be sent and summed in bfloat16 or wider, within the bound.
A program may use at most 64 MiB of HBM per device.

```python
import math
import jax
import jax.numpy as jnp
import numpy as np
from jax import lax

D = 4096
FF = 1024
EXPERTS = 4
TOP = 1
MB_DEV = 16
CAP = 5
HID_DEV = 128
TOKENS_MB = 512
N_SECTION = 16
N_EXPERT = 32


def level_of(stream_key, extent, shards, smallest, top_value):
    loudness, own = 1.0, jax.random.fold_in(stream_key, 6)
    for axis_at, blocks in shards:
        draws = jnp.exp(jax.random.uniform(jax.random.fold_in(own, axis_at), (blocks,), jnp.float32, smallest / len(shards), top_value / len(shards)))
        loudness = loudness * jnp.repeat(draws, extent[axis_at] // blocks).reshape([-1 if axis == axis_at else 1 for axis in range(len(extent))])
    return loudness


def shared_out(own_key, own, number, rows, amount, top, most, lean):
    sequence = jax.random.permutation(own_key, amount)
    crowded, common = shares(amount, rows * top, most, lean, True), shares(amount, rows * top, most, lean, False)
    places = jnp.arange(amount)

    def named(sizes, rotation):
        used = int((sizes > 0).sum())
        fixed = max(1, used // 4)
        passed = fixed + (places - fixed + rotation * (used - fixed)) % max(1, amount - fixed)
        return jnp.zeros((amount,), jnp.int32).at[sequence[jnp.where(places < fixed, places, passed)]].set(jnp.asarray(sizes, jnp.int32))

    sizes = jnp.where(number % 4 == 0, named(crowded, number // 4), named(common, number - number // 4 - 1))
    mixed = jax.random.permutation(jax.random.fold_in(own, 3), amount)
    source_of, sink = mixed[0:amount // 2 * 2:2], mixed[1:amount // 2 * 2:2]
    slack = jnp.minimum(sizes[source_of] - 1, most - sizes[sink]) // 2
    slack = jnp.where((source_of == sequence[0]) | (sink == sequence[0]) | (sizes[sink] == 0), 0, jnp.maximum(slack, 0))
    passed = jax.random.randint(jax.random.fold_in(own, 4), (amount // 2,), 0, 1 << 20) % (slack + 1)
    sizes = sizes.at[source_of].add(-passed).at[sink].add(passed)
    members = jnp.searchsorted(jnp.cumsum(sizes), jnp.arange(rows * top), side="right").astype(jnp.int32)
    table = members.reshape(top, rows).T
    table = table[jax.random.permutation(jax.random.fold_in(own, 1), rows)]
    rotation = jax.random.randint(jax.random.fold_in(own, 2), (rows, 1), 0, top)
    return jnp.take_along_axis(table, (jnp.arange(top)[None, :] + rotation) % top, axis=1)


def shares(count, total, limit, lean, full):
    portions = [(1 << 20) // math.isqrt(rank ** lean) + 1 for rank in range(1, count + 1)]
    largest = limit if full else min(limit, max(-(-total // count), total * portions[0] // sum(portions)))
    least = 1 if total - largest >= count - 1 else 0
    given, surplus = [largest] + [least] * (count - 1), total - largest - least * (count - 1)
    while surplus > 0:
        free = [i for i in range(1, count) if given[i] < largest] or [i for i in range(1, count) if given[i] < limit]
        pool, remaining = sum([portions[i] for i in free]), surplus
        for i in free:
            extra = min(limit - given[i], max(1, remaining * portions[i] // pool), surplus)
            given[i] = given[i] + extra
            surplus = surplus - extra
    return np.array(given)


def bell_draw(own_key, shape, scale, reach, split=(), held_as=jnp.bfloat16):
    loudness = level_of(own_key, shape, split, -0.22, 0.18) if split else 1.0
    array = jax.random.normal(own_key, shape, jnp.float32) * scale * loudness
    return jnp.minimum(jnp.maximum(array, -reach), reach).astype(held_as)


def setup_inputs(seed: int = 0) -> dict:
    splits = jax.random.split(jax.random.key(seed), 10)
    tokens = bell_draw(splits[0], (N_SECTION, TOKENS_MB, D), 1.0, 6.0, ((0, 16), (1, 32)))
    norm_gain = jnp.clip(1.0 + 0.18 * jax.random.normal(splits[1], (N_SECTION, D), jnp.float32), 0.1, 1.9)
    first_routes_keys = jax.random.split(jax.random.fold_in(splits[2], 1), N_SECTION * TOKENS_MB // MB_DEV)
    first_routes_turns = jax.random.permutation(jax.random.fold_in(splits[2], 3), N_SECTION * TOKENS_MB // MB_DEV)
    first_routes = jax.vmap(lambda own, number: shared_out(jax.random.fold_in(splits[2], 2), own, number, MB_DEV, EXPERTS, TOP, CAP, 2))(first_routes_keys, first_routes_turns).reshape((N_SECTION, TOKENS_MB, TOP))
    first_gates = jnp.clip(jnp.exp(math.log(2.0) - 2.0794415 * jax.random.uniform(splits[3], (N_SECTION, TOKENS_MB, TOP), jnp.float32) ** level_of(splits[3], (N_SECTION, TOKENS_MB, TOP), ((0, 16), (1, 32)), -0.2, 0.2)), 0.25, 2.0)
    second_routes_keys = jax.random.split(jax.random.fold_in(splits[4], 1), N_SECTION * TOKENS_MB // MB_DEV)
    second_routes_turns = jax.random.permutation(jax.random.fold_in(splits[4], 3), N_SECTION * TOKENS_MB // MB_DEV)
    second_routes = jax.vmap(lambda own, number: shared_out(jax.random.fold_in(splits[4], 2), own, number, MB_DEV, EXPERTS, TOP, CAP, 2))(second_routes_keys, second_routes_turns).reshape((N_SECTION, TOKENS_MB, TOP))
    second_gates = jnp.clip(jnp.exp(math.log(2.0) - 2.0794415 * jax.random.uniform(splits[5], (N_SECTION, TOKENS_MB, TOP), jnp.float32) ** level_of(splits[5], (N_SECTION, TOKENS_MB, TOP), ((0, 16), (1, 32)), -0.2, 0.2)), 0.25, 2.0)
    gate_proj = bell_draw(splits[6], (N_SECTION, N_EXPERT, D, HID_DEV), D ** -0.5, 0.09375, ((0, 16), (1, 32)))
    up_proj = bell_draw(splits[7], (N_SECTION, N_EXPERT, D, HID_DEV), D ** -0.5, 0.09375, ((0, 16), (1, 32)))
    down_proj = bell_draw(splits[8], (N_SECTION, N_EXPERT, HID_DEV, D), FF ** -0.5, 0.1875, ((0, 16), (1, 32)))
    return {"tokens": tokens, "norm_gain": norm_gain, "first_routes": first_routes, "first_gates": first_gates, "second_routes": second_routes, "second_gates": second_gates, "gate_proj": gate_proj, "up_proj": up_proj, "down_proj": down_proj}


EPS = 1e-06

def normalize(activations, norm_scale):
    values = activations.astype(jnp.float32)
    inv_scale = lax.rsqrt(lax.optimization_barrier(jnp.mean(values * values, axis=-1, keepdims=True)) + EPS)
    return (values * inv_scale * norm_scale.astype(jnp.float32)[None, :]).astype(jnp.bfloat16)

def section_layer(section_args):
    activations, norm_scale, routes, gate_weight, w_gate, w_up, w_down = section_args
    group_size = N_EXPERT // EXPERTS
    row_count = activations.shape[0]
    slot_total = N_EXPERT * CAP
    normed = normalize(activations, norm_scale)
    padded = jnp.concatenate([normed, jnp.zeros((1, D), jnp.bfloat16)], axis=0)
    chosen = routes[:, 0]
    row_order = jnp.arange(row_count, dtype=jnp.int32)
    combined = jnp.zeros((row_count, D), jnp.float32)
    for expert in range(EXPERTS):
        chosen_mask = (chosen == expert).astype(jnp.int32)
        slot_place = jnp.cumsum(chosen_mask) - 1
        target = jnp.where(chosen_mask > 0, slot_place, slot_total).astype(jnp.int32)
        slot_rows = jnp.full((slot_total,), row_count, jnp.int32).at[target].set(row_order, mode='drop')
        picked = padded[slot_rows]
        summed = jnp.zeros((slot_total, D), jnp.float32)
        for slice_index in range(group_size):
            weight_row = expert * group_size + slice_index
            gate_val = jnp.dot(picked, w_gate[weight_row], preferred_element_type=jnp.float32)
            up_val = jnp.dot(picked, w_up[weight_row], preferred_element_type=jnp.float32)
            hidden = (jax.nn.silu(gate_val) * up_val).astype(jnp.bfloat16)
            partial_value = jnp.dot(hidden, w_down[weight_row], preferred_element_type=jnp.float32).astype(jnp.bfloat16)
            summed = summed + lax.optimization_barrier(partial_value).astype(jnp.float32)
        combined = combined.at[slot_rows].add(summed, mode='drop')
    update = (gate_weight[:, 0:1] * combined).astype(jnp.bfloat16)
    update = lax.optimization_barrier(update)
    return (activations.astype(jnp.float32) + update.astype(jnp.float32)).astype(jnp.bfloat16)

def reference(tokens, norm_gain, first_routes, first_gates, second_routes, second_gates, gate_proj, up_proj, down_proj):
    first_pass = lax.map(section_layer, (tokens, norm_gain, first_routes, first_gates, gate_proj, up_proj, down_proj))
    carried = jnp.roll(first_pass, 1, axis=0)
    return lax.map(section_layer, (carried, norm_gain, second_routes, second_gates, gate_proj, up_proj, down_proj))
```

```python
import functools

import jax
import jax.numpy as jnp
from jax import lax
from jax.experimental import pallas as pl
from jax.experimental.pallas import tpu as pltpu
from jax.sharding import PartitionSpec as P

EXPERTS = 4
CAP = 5
EPS = 1e-06
FOLD = 16
MESH = pl.DeviceIdType.MESH

PER_SOURCE = ("yr", "yl", "m0", "rr", "m1", "rl", "m2", "m3", "c1", "s1r", "s1l", "s2r", "s2l")
ONCE = ("za", "zb", "zc", "zd", "ze", "zf", "ra", "rb", "rc", "rd", "re", "rf")
SEMS = {}
for _name in ONCE:
    SEMS[_name, 0] = len(SEMS)
for _name in PER_SOURCE:
    for _k in range(EXPERTS):
        SEMS[_name, _k] = len(SEMS)


def routing(routes_ref):
    rows = routes_ref.shape[0]
    cells = FOLD * rows
    slots = EXPERTS * CAP
    route = routes_ref[...]
    row = lax.broadcasted_iota(jnp.int32, (rows, cells), 0)
    lane = lax.broadcasted_iota(jnp.int32, (rows, cells), 1)
    token = lane & (rows - 1)
    route_f = route.astype(jnp.float32)
    route_lane = jnp.sum(jnp.where(row == token, route_f, 0.0), axis=0, keepdims=True)
    same = route_f == route_lane
    rank_lane = jnp.sum(jnp.where(same & (row < token), 1.0, 0.0), axis=0, keepdims=True)
    rank_row = jnp.sum(jnp.where(same & (lane < row), 1.0, 0.0), axis=1, keepdims=True)
    slot_lane = (route_lane * CAP + rank_lane).astype(jnp.int32)
    slot_row = (route_f * CAP + rank_row).astype(jnp.int32)
    out = lax.broadcasted_iota(jnp.int32, (slots * FOLD, cells), 0)
    cell = lax.broadcasted_iota(jnp.int32, (slots * FOLD, cells), 1)
    pack = ((out >> 4) == slot_lane) & ((out & 15) == (cell >> 4))
    cell = lax.broadcasted_iota(jnp.int32, (cells, slots * FOLD), 0)
    out = lax.broadcasted_iota(jnp.int32, (cells, slots * FOLD), 1)
    slot_cell = jnp.concatenate([slot_row] * FOLD, axis=0)
    unpack = ((out >> 4) == slot_cell) & ((out & 15) == (cell >> 4))
    as_bf16 = lambda mask: jnp.where(mask, 1.0, 0.0).astype(jnp.bfloat16)
    return as_bf16(pack), as_bf16(unpack)


def transposer():
    i = lax.broadcasted_iota(jnp.int32, (FOLD * FOLD, FOLD * FOLD), 0)
    j = lax.broadcasted_iota(jnp.int32, (FOLD * FOLD, FOLD * FOLD), 1)
    hit = ((i >> 4) == (j & 15)) & ((i & 15) == (j >> 4))
    return jnp.where(hit, 1.0, 0.0).astype(jnp.bfloat16)


def dot(a, b):
    return jnp.dot(a, b, preferred_element_type=jnp.float32)


def kernel(
    n_section, x_ref, gain_ref, r1_ref, g1_ref, r2_ref, g2_ref, wg_ref, wu_ref, wd_ref, out_ref,
    wgu, wd, sent, zr, box, flat, stack, parts, core_in, chip_sum, y_one, v_right, v_left, y_two,
    final, zq, back, first, carried, w_sem, send_sem, recv_sem, shift_sem,
):
    rows, depth = x_ref.shape
    width = depth // FOLD
    half = width // 2
    hidden_units = wd.shape[0]
    me = lax.axis_index("expert")
    e, y, c = me // 8, (me // 2) % 4, me % 2
    e1, e2, e3 = (e + 1) % 4, (e + 2) % 4, (e + 3) % 4
    y1, y2, y3 = (y + 1) % 4, (y + 2) % 4, (y + 3) % 4
    oc = 1 - c
    up, down = e1 * 8 + y * 2 + c, e3 * 8 + y * 2 + c
    right, left = e * 8 + y1 * 2 + c, e * 8 + y3 * 2 + c
    mate = e * 8 + y * 2 + oc
    section = lax.axis_index("section")
    after, before = (section + 1) % n_section, (section + n_section - 1) % n_section

    barrier = pltpu.get_barrier_semaphore()
    for peer in (up, down, right, left, mate):
        pl.semaphore_signal(barrier, inc=1, device_id={"expert": peer}, device_id_type=MESH)
    if n_section > 1:
        for peer in (after, before):
            pl.semaphore_signal(barrier, inc=1, device_id={"section": peer}, device_id_type=MESH)

    loads = [
        pltpu.make_async_copy(wg_ref, wgu.at[:, pl.ds(0, hidden_units)], w_sem.at[0]),
        pltpu.make_async_copy(wu_ref, wgu.at[:, pl.ds(hidden_units, hidden_units)], w_sem.at[1]),
        pltpu.make_async_copy(wd_ref, wd, w_sem.at[2]),
    ]
    for load in loads:
        load.start()

    def base(c_, e_, y_):
        return ((c_ * 4 + e_) * 4 + y_) * CAP

    def one_round(r, act_ref, routes_ref, gates_ref, result_ref):
        started = []
        box_r = box.at[r]
        back_r = back.at[r]

        def send(name, src, dst, peer, k=0):
            i = SEMS[name, k]
            copy = pltpu.make_async_remote_copy(
                src_ref=src, dst_ref=dst, send_sem=send_sem.at[i], recv_sem=recv_sem.at[r, i],
                device_id={"expert": peer}, device_id_type=MESH,
            )
            copy.start()
            started.append(copy)

        def arrived(name, dst, k=0):
            i = SEMS[name, k]
            pltpu.make_async_remote_copy(
                src_ref=dst, dst_ref=dst, send_sem=send_sem.at[i], recv_sem=recv_sem.at[r, i],
                device_id={"expert": mate}, device_id_type=MESH,
            ).wait_recv()

        def five(ref, h, start):
            return ref.at[pl.ds(0, 2) if h is None else h, pl.ds(start, CAP)]

        def place(h, c_, e_, y_):
            return five(box_r, h, base(c_, e_, y_))

        values = act_ref[...].astype(jnp.float32)
        scale = lax.rsqrt(jnp.mean(values * values, axis=-1, keepdims=True) + EPS)
        normed = (values * scale * gain_ref[...]).astype(jnp.bfloat16)
        pack, unpack = routing(routes_ref)
        tall = jnp.concatenate([normed[:, f * width:(f + 1) * width] for f in range(FOLD)], axis=0)
        packed = dot(pack, tall).astype(jnp.bfloat16)
        for h in range(2):
            sent[h] = packed[:, h * half:(h + 1) * half].reshape(EXPERTS * CAP, FOLD, half)
        if r == 0:
            pl.semaphore_wait(barrier, 7 if n_section > 1 else 5)

        send("za", five(sent, 0, e2 * CAP), zr.at[r, 0], up)
        send("zb", five(sent, 1, e2 * CAP), zr.at[r, 1], down)
        send("zc", five(sent, None, e1 * CAP), place(None, c, e, y), up)
        send("zd", five(sent, None, e3 * CAP), place(None, c, e, y), down)
        own = base(c, e, y)
        box[r, :, pl.ds(own, CAP)] = sent[:, pl.ds(e * CAP, CAP)]

        source = {0: e, 1: e1, 2: e2, 3: e3}

        def y_send(k):
            piece = place(None, c, source[k], y)
            send("yr", piece, piece, right, k)
            send("yl", piece, piece, left, k)
            send("m0", piece, piece, mate, k)

        def y_relay(k):
            s = source[k]
            arrived("yr", place(None, c, s, y3), k)
            send("rr", place(0, c, s, y3), place(0, c, s, y3), right, k)
            send("m1", place(None, c, s, y3), place(None, c, s, y3), mate, k)
            arrived("yl", place(None, c, s, y1), k)
            send("rl", place(1, c, s, y1), place(1, c, s, y1), left, k)
            send("m2", place(None, c, s, y1), place(None, c, s, y1), mate, k)

        def y_last(k):
            s = source[k]
            arrived("rr", place(0, c, s, y2), k)
            arrived("rl", place(1, c, s, y2), k)
            send("m3", place(None, c, s, y2), place(None, c, s, y2), mate, k)

        y_send(0)
        y_relay(0)
        y_last(0)
        arrived("za", zr.at[r, 0])
        send("ze", zr.at[r, 0], place(0, c, e3, y), up)
        arrived("zb", zr.at[r, 1])
        send("zf", zr.at[r, 1], place(1, c, e1, y), down)
        arrived("zc", place(None, c, e3, y))
        y_send(3)
        arrived("zd", place(None, c, e1, y))
        y_send(1)
        for k in (3, 1):
            y_relay(k)
        for k in (3, 1):
            y_last(k)
        arrived("ze", place(0, c, e2, y))
        arrived("zf", place(1, c, e2, y))
        y_send(2)
        y_relay(2)
        y_last(2)
        for k in (0, 3, 1, 2):
            s = source[k]
            for name, y_ in (("m0", y), ("m1", y3), ("m2", y1), ("m3", y2)):
                arrived(name, place(None, oc, s, y_), k)

        if r == 0:
            for load in loads:
                load.wait()
        swap = transposer()
        groups = flat.shape[0] // FOLD
        for g in range(groups):
            block = jnp.concatenate(
                [box[r, h, g * FOLD:(g + 1) * FOLD].reshape(FOLD * FOLD, half) for h in range(2)], axis=1
            )
            block = dot(swap, block).astype(jnp.bfloat16)
            for f in range(FOLD):
                flat[g * FOLD:(g + 1) * FOLD, f * width:(f + 1) * width] = block[f * FOLD:(f + 1) * FOLD]
        both = dot(flat[...], wgu[...])
        gate_val, up_val = both[:, :hidden_units], both[:, hidden_units:]
        hidden = (gate_val / (1.0 + jnp.exp(-gate_val)) * up_val).astype(jnp.bfloat16)
        for f in range(FOLD):
            column = dot(hidden, wd[:, f * width:(f + 1) * width]).astype(jnp.bfloat16)
            for g in range(groups):
                stack[g, f * FOLD:(f + 1) * FOLD] = column[g * FOLD:(g + 1) * FOLD]
        for g in range(groups):
            block = dot(swap, stack[g]).astype(jnp.bfloat16)
            for h in range(2):
                parts[h, g * FOLD:(g + 1) * FOLD] = block[:, h * half:(h + 1) * half].reshape(FOLD, FOLD, half)

        order = (2, 1, 3, 0)
        wide = 4 * CAP
        for k in order:
            send("c1", parts.at[:, pl.ds(base(oc, source[k], 0), wide)], core_in.at[r, k], mate, k)
        for k in order:
            arrived("c1", core_in.at[r, k], k)
            mine = parts[:, pl.ds(base(c, source[k], 0), wide)].astype(jnp.float32)
            chip_sum[k] = (mine + core_in[r, k].astype(jnp.float32)).astype(jnp.bfloat16)
            send("s1r", chip_sum.at[k, 0, pl.ds(y2 * CAP, CAP)], y_one.at[r, 0, k], right, k)
            send("s1l", chip_sum.at[k, 1, pl.ds(y2 * CAP, CAP)], y_one.at[r, 1, k], left, k)
        for k in order:
            for name, h, y_, buf, peer, out in (("s1r", 0, y1, v_right, right, "s2r"), ("s1l", 1, y3, v_left, left, "s2l")):
                arrived(name, y_one.at[r, h, k], k)
                mine = chip_sum[k, h, pl.ds(y_ * CAP, CAP)].astype(jnp.float32)
                buf[k, h] = (mine + y_one[r, h, k].astype(jnp.float32)).astype(jnp.bfloat16)
                buf[k, 1 - h] = chip_sum[k, 1 - h, pl.ds(y_ * CAP, CAP)]
                send(out, buf.at[k], y_two.at[r, h, k], peer, k)
        for k in order:
            arrived("s2r", y_two.at[r, 0, k], k)
            arrived("s2l", y_two.at[r, 1, k], k)
            total = chip_sum[k, :, pl.ds(y * CAP, CAP)].astype(jnp.float32)
            total = total + y_two[r, 0, k].astype(jnp.float32) + y_two[r, 1, k].astype(jnp.float32)
            if k == 0:
                back[r, :, pl.ds(e * CAP, CAP)] = total.astype(jnp.bfloat16)
            else:
                final[k] = total.astype(jnp.bfloat16)
            if k == 2:
                send("ra", final.at[2, 0], zq.at[r, 0], up)
                send("rb", final.at[2, 1], zq.at[r, 1], down)
            if k == 1:
                send("rc", final.at[1], five(back_r, None, e * CAP), up)
            if k == 3:
                send("rd", final.at[3], five(back_r, None, e * CAP), down)
        arrived("ra", zq.at[r, 0])
        send("re", zq.at[r, 0], five(back_r, 0, e3 * CAP), up)
        arrived("rb", zq.at[r, 1])
        send("rf", zq.at[r, 1], five(back_r, 1, e1 * CAP), down)
        arrived("rc", five(back_r, None, e3 * CAP))
        arrived("rd", five(back_r, None, e1 * CAP))
        arrived("re", five(back_r, 0, e2 * CAP))
        arrived("rf", five(back_r, 1, e2 * CAP))

        got = jnp.concatenate([back[r, h].reshape(EXPERTS * CAP * FOLD, half) for h in range(2)], axis=1)
        got = dot(unpack, got)
        got = jnp.concatenate([got[f * rows:(f + 1) * rows] for f in range(FOLD)], axis=1)
        update = (gates_ref[...] * got).astype(jnp.bfloat16)
        result_ref[...] = (act_ref[...].astype(jnp.float32) + update.astype(jnp.float32)).astype(jnp.bfloat16)
        for copy in started:
            copy.wait_send()

    one_round(0, x_ref, r1_ref, g1_ref, first)
    if n_section > 1:
        shift = pltpu.make_async_remote_copy(
            src_ref=first, dst_ref=carried, send_sem=shift_sem.at[0], recv_sem=shift_sem.at[1],
            device_id={"section": after}, device_id_type=MESH,
        )
        shift.start()
        shift.wait()
        one_round(1, carried, r2_ref, g2_ref, out_ref)
    else:
        one_round(1, first, r2_ref, g2_ref, out_ref)


def on_device(n_section, tokens, norm_gain, first_routes, first_gates, second_routes, second_gates, gate_proj, up_proj, down_proj):
    rows, depth = tokens.shape[1:]
    units = gate_proj.shape[-1]
    half = depth // FOLD // 2
    slots = lax.axis_size("expert") * CAP
    bf16 = jnp.bfloat16
    near = pl.BlockSpec(memory_space=pltpu.VMEM)
    far = pl.BlockSpec(memory_space=pl.ANY)
    return pl.pallas_call(
        functools.partial(kernel, n_section),
        out_shape=jax.ShapeDtypeStruct((rows, depth), bf16),
        in_specs=[near] * 6 + [far] * 3,
        out_specs=near,
        scratch_shapes=[
            pltpu.VMEM((depth, 2 * units), bf16),
            pltpu.VMEM((units, depth), bf16),
            pltpu.VMEM((2, EXPERTS * CAP, FOLD, half), bf16),
            pltpu.VMEM((2, 2, CAP, FOLD, half), bf16),
            pltpu.VMEM((2, 2, slots, FOLD, half), bf16),
            pltpu.VMEM((slots, depth), bf16),
            pltpu.VMEM((slots // FOLD, FOLD * FOLD, depth // FOLD), bf16),
            pltpu.VMEM((2, slots, FOLD, half), bf16),
            pltpu.VMEM((2, 4, 2, 4 * CAP, FOLD, half), bf16),
            pltpu.VMEM((4, 2, 4 * CAP, FOLD, half), bf16),
            pltpu.VMEM((2, 2, 4, CAP, FOLD, half), bf16),
            pltpu.VMEM((4, 2, CAP, FOLD, half), bf16),
            pltpu.VMEM((4, 2, CAP, FOLD, half), bf16),
            pltpu.VMEM((2, 2, 4, 2, CAP, FOLD, half), bf16),
            pltpu.VMEM((4, 2, CAP, FOLD, half), bf16),
            pltpu.VMEM((2, 2, CAP, FOLD, half), bf16),
            pltpu.VMEM((2, 2, EXPERTS * CAP, FOLD, half), bf16),
            pltpu.VMEM((rows, depth), bf16),
            pltpu.VMEM((rows, depth), bf16),
            pltpu.SemaphoreType.DMA((3,)),
            pltpu.SemaphoreType.DMA((len(SEMS),)),
            pltpu.SemaphoreType.DMA((2, len(SEMS))),
            pltpu.SemaphoreType.DMA((2,)),
        ],
        compiler_params=pltpu.CompilerParams(collective_id=0, has_side_effects=True),
    )(
        tokens[0], norm_gain, first_routes[0], first_gates[0], second_routes[0], second_gates[0],
        gate_proj[0, 0], up_proj[0, 0], down_proj[0, 0],
    )[None]


def solution(mesh):
    rows = P("section", "expert", None)
    weights = P("section", "expert", None, None)
    return jax.shard_map(
        functools.partial(on_device, mesh.shape["section"]),
        mesh=mesh,
        in_specs=(rows, P("section", None), rows, rows, rows, rows, weights, weights, weights),
        out_specs=rows,
        check_vma=False,
    )
```

```python
import functools

import jax
import jax.numpy as jnp
from jax import lax
from jax.experimental import pallas as pl
from jax.experimental.pallas import tpu as pltpu
from jax.sharding import PartitionSpec as P

EXPERTS = 4
CAP = 5
EPS = 1e-06
FOLD = 16
MESH = pl.DeviceIdType.MESH

PER_SOURCE = ("yr", "yl", "ya", "m0", "m1", "m2", "m3", "c1", "sr", "sl", "sa")
ONCE = ("zc", "zd", "zf", "rc", "rd", "rf", "ro", "tok", "inf")
SEMS = {}
for _name in ONCE:
    SEMS[_name, 0] = len(SEMS)
for _name in PER_SOURCE:
    for _k in range(EXPERTS):
        SEMS[_name, _k] = len(SEMS)


def column(lane_values):
    n = lane_values.shape[1]
    row = lax.broadcasted_iota(jnp.int32, (n, n), 0)
    lane = lax.broadcasted_iota(jnp.int32, (n, n), 1)
    return jnp.sum(jnp.where(row == lane, lane_values, 0.0), axis=1, keepdims=True)


def slots_of(route_lanes):
    rows = route_lanes.shape[1]
    route_row = column(route_lanes)
    row = lax.broadcasted_iota(jnp.int32, (rows, FOLD * rows), 0)
    lane = lax.broadcasted_iota(jnp.int32, (rows, FOLD * rows), 1)
    token = lane & (rows - 1)
    route_lane = jnp.sum(jnp.where(row == token, route_row, 0.0), axis=0, keepdims=True)
    same = route_row == route_lane
    rank_lane = jnp.sum(jnp.where(same & (row < token), 1.0, 0.0), axis=0, keepdims=True)
    rank_row = jnp.sum(jnp.where(same & (lane < row), 1.0, 0.0), axis=1, keepdims=True)
    return (route_lane * CAP + rank_lane).astype(jnp.int32), (route_row * CAP + rank_row).astype(jnp.int32)


def packer(route_lanes):
    shape = (EXPERTS * CAP * FOLD, FOLD * route_lanes.shape[1])
    slot_lane, _ = slots_of(route_lanes)
    out = lax.broadcasted_iota(jnp.int32, shape, 0)
    cell = lax.broadcasted_iota(jnp.int32, shape, 1)
    hit = ((out >> 4) == slot_lane) & ((out & 15) == (cell >> 4))
    return jnp.where(hit, 1.0, 0.0).astype(jnp.bfloat16)


def unpacker(route_lanes):
    shape = (FOLD * route_lanes.shape[1], EXPERTS * CAP * FOLD)
    _, slot_row = slots_of(route_lanes)
    cell = lax.broadcasted_iota(jnp.int32, shape, 0)
    out = lax.broadcasted_iota(jnp.int32, shape, 1)
    slot_cell = jnp.concatenate([slot_row] * FOLD, axis=0)
    hit = ((out >> 4) == slot_cell) & ((out & 15) == (cell >> 4))
    return jnp.where(hit, 1.0, 0.0).astype(jnp.bfloat16)


def transposer():
    i = lax.broadcasted_iota(jnp.int32, (FOLD * FOLD, FOLD * FOLD), 0)
    j = lax.broadcasted_iota(jnp.int32, (FOLD * FOLD, FOLD * FOLD), 1)
    hit = ((i >> 4) == (j & 15)) & ((i & 15) == (j >> 4))
    return jnp.where(hit, 1.0, 0.0).astype(jnp.bfloat16)


def dot(a, b):
    return jnp.dot(a, b, preferred_element_type=jnp.float32)


START = {0: 0, 1: 48, 3: 88, 2: 128}
SLOTS = 176


def kernel(
    n_section, x_ref, gain_ref, r1_ref, g1_ref, r2_ref, g2_ref, wg_ref, wu_ref, wd_ref, out_ref,
    wgu, wd, sent, box, flat, stack, parts, core_in, chip_sum, y_in, final, back, tokens_in, info, info_in, carried, pack_m, unpack_m, swap_m, w_sem, send_sem, recv_sem,
):
    rows, depth = x_ref.shape
    width = depth // FOLD
    half = width // 2
    hidden_units = wd.shape[0]
    me = lax.axis_index("expert")
    e, y, c = me // 8, (me // 2) % 4, me % 2
    e1, e2, e3 = (e + 1) % 4, (e + 2) % 4, (e + 3) % 4
    y1, y2, y3 = (y + 1) % 4, (y + 2) % 4, (y + 3) % 4
    oc = 1 - c
    up, down = e1 * 8 + y * 2 + c, e3 * 8 + y * 2 + c
    right, left = e * 8 + y1 * 2 + c, e * 8 + y3 * 2 + c
    far, across, mate = e2 * 8 + y * 2 + c, e * 8 + y2 * 2 + c, e * 8 + y * 2 + oc
    section = lax.axis_index("section")
    after, before = (section + 1) % n_section, (section + n_section - 1) % n_section

    barrier = pltpu.get_barrier_semaphore()
    for peer in (up, down, far, right, left, across, mate):
        pl.semaphore_signal(barrier, inc=1, device_id={"expert": peer}, device_id_type=MESH)
    for other in (after, before):
        for peer in (me, up, down, far):
            pl.semaphore_signal(barrier, inc=1, device_id={"section": other, "expert": peer}, device_id_type=MESH)

    loads = [
        pltpu.make_async_copy(wg_ref, wgu.at[:, pl.ds(0, hidden_units)], w_sem.at[0]),
        pltpu.make_async_copy(wu_ref, wgu.at[:, pl.ds(hidden_units, hidden_units)], w_sem.at[1]),
        pltpu.make_async_copy(wd_ref, wd, w_sem.at[2]),
    ]
    for load in loads:
        load.start()

    def base(c_, k, y_):
        return START[k] + (c_ * 4 + y_) * CAP

    def one_round(r, act_ref, routes_ref, gates_ref, result_ref):
        started = []
        home = after if r == 0 else None
        box_r = box.at[r]
        back_r = back.at[r]

        def send(name, src, dst, peer, k=0, to=None):
            i = SEMS[name, k]
            copy = pltpu.make_async_remote_copy(
                src_ref=src, dst_ref=dst, send_sem=send_sem.at[i], recv_sem=recv_sem.at[r, i],
                device_id={"expert": peer} if to is None else {"section": to, "expert": peer}, device_id_type=MESH,
            )
            copy.start()
            started.append(copy)

        def arrived(name, dst, k=0):
            i = SEMS[name, k]
            pltpu.make_async_remote_copy(
                src_ref=dst, dst_ref=dst, send_sem=send_sem.at[i], recv_sem=recv_sem.at[r, i],
                device_id={"expert": mate}, device_id_type=MESH,
            ).wait_recv()

        def five(ref, h, start):
            return ref.at[pl.ds(0, 2) if h is None else h, pl.ds(start, CAP)]

        def place(h, c_, k, y_):
            return five(box_r, h, base(c_, k, y_))

        values = act_ref[...].astype(jnp.float32)
        scale = lax.rsqrt(jnp.mean(values * values, axis=-1, keepdims=True) + EPS)
        normed = (values * scale * gain_ref[...]).astype(jnp.bfloat16)
        if r == 0:
            pack_m[0] = packer(routes_ref[...].astype(jnp.float32))
        tall = jnp.concatenate([normed[:, f * width:(f + 1) * width] for f in range(FOLD)], axis=0)
        packed = dot(pack_m[r], tall).astype(jnp.bfloat16)
        for h in range(2):
            sent[h] = packed[:, h * half:(h + 1) * half].reshape(EXPERTS * CAP, FOLD, half)
        if r == 0:
            pl.semaphore_wait(barrier, 15)

        send("zf", five(sent, None, e2 * CAP), place(None, c, 2, y), far)
        send("zc", five(sent, None, e1 * CAP), place(None, c, 3, y), up)
        send("zd", five(sent, None, e3 * CAP), place(None, c, 1, y), down)

        def y_send(k):
            piece = place(None, c, k, y)
            src = piece if k else five(sent, None, e * CAP)
            send("yr", src, piece, right, k)
            send("yl", src, piece, left, k)
            send("ya", src, piece, across, k)
            send("m0", src, piece, mate, k)

        def y_near(k):
            arrived("yr", place(None, c, k, y3), k)
            send("m1", place(None, c, k, y3), place(None, c, k, y3), mate, k)
            arrived("yl", place(None, c, k, y1), k)
            send("m2", place(None, c, k, y1), place(None, c, k, y1), mate, k)

        def y_last(k):
            arrived("ya", place(None, c, k, y2), k)
            send("m3", place(None, c, k, y2), place(None, c, k, y2), mate, k)

        def gathered(k):
            for name, y_ in (("m0", y), ("m1", y3), ("m2", y1), ("m3", y2)):
                arrived(name, place(None, oc, k, y_), k)

        def experts(lo, hi):
            groups = range(lo // FOLD, hi // FOLD)
            swap = swap_m[...]
            for g in groups:
                block = jnp.concatenate(
                    [box[r, h, g * FOLD:(g + 1) * FOLD].reshape(FOLD * FOLD, half) for h in range(2)], axis=1
                )
                block = dot(swap, block).astype(jnp.bfloat16)
                for f in range(FOLD):
                    flat[g * FOLD:(g + 1) * FOLD, f * width:(f + 1) * width] = block[f * FOLD:(f + 1) * FOLD]
            both = dot(flat[lo:hi], wgu[...])
            gate_val, up_val = both[:, :hidden_units], both[:, hidden_units:]
            hidden = (gate_val / (1.0 + jnp.exp(-gate_val)) * up_val).astype(jnp.bfloat16)
            for f in range(FOLD):
                piece = dot(hidden, wd[:, f * width:(f + 1) * width]).astype(jnp.bfloat16)
                for g in groups:
                    stack[g, f * FOLD:(f + 1) * FOLD] = piece[g * FOLD - lo:(g + 1) * FOLD - lo]
            for g in groups:
                block = dot(swap, stack[g]).astype(jnp.bfloat16)
                for h in range(2):
                    parts[h, g * FOLD:(g + 1) * FOLD] = block[:, h * half:(h + 1) * half].reshape(FOLD, FOLD, half)

        wide = 4 * CAP

        def to_mate(k):
            send("c1", parts.at[:, pl.ds(base(oc, k, 0), wide)], core_in.at[r, k], mate, k)

        def sum_cores(k):
            arrived("c1", core_in.at[r, k], k)
            mine = parts[:, pl.ds(base(c, k, 0), wide)].astype(jnp.float32)
            chip_sum[k] = (mine + core_in[r, k].astype(jnp.float32)).astype(jnp.bfloat16)
            for name, y_, peer, at in (("sa", y2, across, 2), ("sr", y1, right, 0), ("sl", y3, left, 1)):
                send(name, chip_sum.at[k, :, pl.ds(y_ * CAP, CAP)], y_in.at[r, at, k], peer, k)

        def sum_all(k):
            total = chip_sum[k, :, pl.ds(y * CAP, CAP)].astype(jnp.float32)
            for at, name in enumerate(("sr", "sl", "sa")):
                arrived(name, y_in.at[r, at, k], k)
                total = total + y_in[r, at, k].astype(jnp.float32)
            if k == 0 and r == 1:
                back[r, :, pl.ds(e * CAP, CAP)] = total.astype(jnp.bfloat16)
            else:
                final[k] = total.astype(jnp.bfloat16)
            if k == 0 and r == 0:
                send("ro", final.at[0], five(back_r, None, e * CAP), me, 0, home)
            if k == 2:
                send("rf", final.at[2], five(back_r, None, e * CAP), far, 0, home)
            if k == 1:
                send("rc", final.at[1], five(back_r, None, e * CAP), up, 0, home)
            if k == 3:
                send("rd", final.at[3], five(back_r, None, e * CAP), down, 0, home)

        y_send(0)
        box[r, :, pl.ds(base(c, 0, y), CAP)] = sent[:, pl.ds(e * CAP, CAP)]
        if r == 0:
            swap_m[...] = transposer()
            pack_m[1] = packer(r2_ref[...].astype(jnp.float32))
            unpack_m[1] = unpacker(r2_ref[...].astype(jnp.float32))
            info[0:1, 0:rows] = routes_ref[...].astype(jnp.float32)
            info[1:2, 0:rows] = gates_ref[...]
            for q in range(2):
                for lo in (40, 168):
                    box[q, :, lo:lo + 8] = jnp.zeros((2, 8, FOLD, half), jnp.bfloat16)
            for load in loads:
                load.wait()
        y_near(0)
        y_last(0)
        gathered(0)
        experts(0, 48)
        to_mate(0)
        arrived("zc", place(None, c, 3, y))
        y_send(3)
        arrived("zd", place(None, c, 1, y))
        y_send(1)
        sum_cores(0)
        y_near(3)
        y_near(1)
        arrived("zf", place(None, c, 2, y))
        y_send(2)
        if r == 0:
            send("tok", act_ref, tokens_in, me, 0, after)
            send("inf", info, info_in, me, 0, after)
        y_last(3)
        y_last(1)
        sum_all(0)
        y_near(2)
        y_last(2)
        gathered(1)
        gathered(3)
        experts(48, 128)
        to_mate(1)
        to_mate(3)
        gathered(2)
        experts(128, 176)
        to_mate(2)
        sum_cores(1)
        sum_cores(3)
        sum_cores(2)
        sum_all(1)
        sum_all(3)
        sum_all(2)
        if r == 0:
            arrived("tok", tokens_in)
            arrived("inf", info_in)
            unpack_m[0] = unpacker(info_in[0:1, 0:rows])
            arrived("ro", five(back_r, None, e * CAP))
        arrived("rc", five(back_r, None, e3 * CAP))
        arrived("rd", five(back_r, None, e1 * CAP))
        arrived("rf", five(back_r, None, e2 * CAP))

        got = jnp.concatenate([back[r, h].reshape(EXPERTS * CAP * FOLD, half) for h in range(2)], axis=1)
        got = dot(unpack_m[r], got)
        got = jnp.concatenate([got[f * rows:(f + 1) * rows] for f in range(FOLD)], axis=1)
        gates, base_ref = (info_in[1:2, 0:rows], tokens_in) if r == 0 else (gates_ref[...], act_ref)
        update = (column(gates) * got).astype(jnp.bfloat16)
        result_ref[...] = (base_ref[...].astype(jnp.float32) + update.astype(jnp.float32)).astype(jnp.bfloat16)
        return started

    started = one_round(0, x_ref, r1_ref, g1_ref, carried)
    for copy in started:
        copy.wait_send()
    started = one_round(1, carried, r2_ref, g2_ref, out_ref)
    for copy in started:
        copy.wait_send()


def on_device(n_section, tokens, norm_gain, first_routes, first_gates, second_routes, second_gates, gate_proj, up_proj, down_proj):
    rows, depth = tokens.shape[1:]
    units = gate_proj.shape[-1]
    half = depth // FOLD // 2
    slots = SLOTS
    cells = FOLD * rows
    bf16 = jnp.bfloat16
    near = pl.BlockSpec(memory_space=pltpu.VMEM)
    far = pl.BlockSpec(memory_space=pl.ANY)
    return pl.pallas_call(
        functools.partial(kernel, n_section),
        out_shape=jax.ShapeDtypeStruct((rows, depth), bf16),
        in_specs=[near] * 6 + [far] * 3,
        out_specs=near,
        scratch_shapes=[
            pltpu.VMEM((depth, 2 * units), bf16),
            pltpu.VMEM((units, depth), bf16),
            pltpu.VMEM((2, EXPERTS * CAP, FOLD, half), bf16),
            pltpu.VMEM((2, 2, slots, FOLD, half), bf16),
            pltpu.VMEM((slots, depth), bf16),
            pltpu.VMEM((slots // FOLD, FOLD * FOLD, depth // FOLD), bf16),
            pltpu.VMEM((2, slots, FOLD, half), bf16),
            pltpu.VMEM((2, 4, 2, 4 * CAP, FOLD, half), bf16),
            pltpu.VMEM((4, 2, 4 * CAP, FOLD, half), bf16),
            pltpu.VMEM((2, 3, 4, 2, CAP, FOLD, half), bf16),
            pltpu.VMEM((4, 2, CAP, FOLD, half), bf16),
            pltpu.VMEM((2, 2, EXPERTS * CAP, FOLD, half), bf16),
            pltpu.VMEM((rows, depth), bf16),
            pltpu.VMEM((8, 128), jnp.float32),
            pltpu.VMEM((8, 128), jnp.float32),
            pltpu.VMEM((rows, depth), bf16),
            pltpu.VMEM((2, EXPERTS * CAP * FOLD, cells), bf16),
            pltpu.VMEM((2, cells, EXPERTS * CAP * FOLD), bf16),
            pltpu.VMEM((FOLD * FOLD, FOLD * FOLD), bf16),
            pltpu.SemaphoreType.DMA((3,)),
            pltpu.SemaphoreType.DMA((len(SEMS),)),
            pltpu.SemaphoreType.DMA((2, len(SEMS))),
        ],
        compiler_params=pltpu.CompilerParams(collective_id=0, has_side_effects=True),
    )(
        tokens[0], norm_gain, *(a.reshape(1, rows) for a in (first_routes, first_gates, second_routes, second_gates)),
        gate_proj[0, 0], up_proj[0, 0], down_proj[0, 0],
    )[None]


def solution(mesh):
    rows = P("section", "expert", None)
    weights = P("section", "expert", None, None)
    return jax.shard_map(
        functools.partial(on_device, mesh.shape["section"]),
        mesh=mesh,
        in_specs=(rows, P("section", None), rows, rows, rows, rows, weights, weights, weights),
        out_specs=rows,
        check_vma=False,
    )
```

```python
import functools

import jax
import jax.numpy as jnp
from jax import lax
from jax.experimental import pallas as pl
from jax.experimental.pallas import tpu as pltpu
from jax.sharding import PartitionSpec as P

EXPERTS = 4
CAP = 5
EPS = 1e-06
FOLD = 16
MESH = pl.DeviceIdType.MESH

PER_SOURCE = ("yr", "yl", "ya", "m0", "m1", "m2", "m3", "c1", "sr", "sl", "sa")
ONCE = ("zc", "zd", "zf", "rc", "rd", "rf", "ro", "tok", "inf")
SEMS = {}
for _name in ONCE:
    SEMS[_name, 0] = len(SEMS)
for _name in PER_SOURCE:
    for _k in range(EXPERTS):
        SEMS[_name, _k] = len(SEMS)


def column(lane_values):
    n = lane_values.shape[1]
    row = lax.broadcasted_iota(jnp.int32, (n, n), 0)
    lane = lax.broadcasted_iota(jnp.int32, (n, n), 1)
    return jnp.sum(jnp.where(row == lane, lane_values, 0.0), axis=1, keepdims=True)


def slots_of(route_lanes):
    rows = route_lanes.shape[1]
    route_row = column(route_lanes)
    row = lax.broadcasted_iota(jnp.int32, (rows, FOLD * rows), 0)
    lane = lax.broadcasted_iota(jnp.int32, (rows, FOLD * rows), 1)
    token = lane & (rows - 1)
    route_lane = jnp.sum(jnp.where(row == token, route_row, 0.0), axis=0, keepdims=True)
    same = route_row == route_lane
    rank_lane = jnp.sum(jnp.where(same & (row < token), 1.0, 0.0), axis=0, keepdims=True)
    rank_row = jnp.sum(jnp.where(same & (lane < row), 1.0, 0.0), axis=1, keepdims=True)
    return (route_lane * CAP + rank_lane).astype(jnp.int32), (route_row * CAP + rank_row).astype(jnp.int32)


def packer(route_lanes):
    shape = (EXPERTS * CAP * FOLD, FOLD * route_lanes.shape[1])
    slot_lane, _ = slots_of(route_lanes)
    out = lax.broadcasted_iota(jnp.int32, shape, 0)
    cell = lax.broadcasted_iota(jnp.int32, shape, 1)
    hit = ((out >> 4) == slot_lane) & ((out & 15) == (cell >> 4))
    return jnp.where(hit, 1.0, 0.0).astype(jnp.bfloat16)


def unpacker(route_lanes):
    shape = (FOLD * route_lanes.shape[1], EXPERTS * CAP * FOLD)
    _, slot_row = slots_of(route_lanes)
    cell = lax.broadcasted_iota(jnp.int32, shape, 0)
    out = lax.broadcasted_iota(jnp.int32, shape, 1)
    slot_cell = jnp.concatenate([slot_row] * FOLD, axis=0)
    hit = ((out >> 4) == slot_cell) & ((out & 15) == (cell >> 4))
    return jnp.where(hit, 1.0, 0.0).astype(jnp.bfloat16)


def transposer():
    i = lax.broadcasted_iota(jnp.int32, (FOLD * FOLD, FOLD * FOLD), 0)
    j = lax.broadcasted_iota(jnp.int32, (FOLD * FOLD, FOLD * FOLD), 1)
    hit = ((i >> 4) == (j & 15)) & ((i & 15) == (j >> 4))
    return jnp.where(hit, 1.0, 0.0).astype(jnp.bfloat16)


def dot(a, b):
    return jnp.dot(a, b, preferred_element_type=jnp.float32)


START = {0: 0, 1: 48, 3: 88, 2: 128}
SLOTS = 176


def kernel(
    n_section, x_ref, gain_ref, r1_ref, g1_ref, r2_ref, g2_ref, wg_ref, wu_ref, wd_ref, out_ref,
    wgu, wd, sent, box, flat, stack, parts, core_in, chip_sum, y_in, final, back, tokens_in, info, info_in, carried, pack_m, unpack_m, swap_m, w_sem, send_sem, recv_sem,
):
    rows, depth = x_ref.shape
    width = depth // FOLD
    half = width // 2
    hidden_units = wd.shape[0]
    me = lax.axis_index("expert")
    e, y, c = me // 8, (me // 2) % 4, me % 2
    e1, e2, e3 = (e + 1) % 4, (e + 2) % 4, (e + 3) % 4
    y1, y2, y3 = (y + 1) % 4, (y + 2) % 4, (y + 3) % 4
    oc = 1 - c
    up, down = e1 * 8 + y * 2 + c, e3 * 8 + y * 2 + c
    right, left = e * 8 + y1 * 2 + c, e * 8 + y3 * 2 + c
    far, across, mate = e2 * 8 + y * 2 + c, e * 8 + y2 * 2 + c, e * 8 + y * 2 + oc
    section = lax.axis_index("section")
    after, before = (section + 1) % n_section, (section + n_section - 1) % n_section

    barrier = pltpu.get_barrier_semaphore()
    for peer in (up, down, far, right, left, across, mate):
        pl.semaphore_signal(barrier, inc=1, device_id={"expert": peer}, device_id_type=MESH)
    for other in (after, before):
        for peer in (me, up, down, far):
            pl.semaphore_signal(barrier, inc=1, device_id={"section": other, "expert": peer}, device_id_type=MESH)

    loads = [
        pltpu.make_async_copy(wg_ref, wgu.at[:, pl.ds(0, hidden_units)], w_sem.at[0]),
        pltpu.make_async_copy(wu_ref, wgu.at[:, pl.ds(hidden_units, hidden_units)], w_sem.at[1]),
        pltpu.make_async_copy(wd_ref, wd, w_sem.at[2]),
    ]
    for load in loads:
        load.start()

    def base(c_, k, y_):
        return START[k] + (c_ * 4 + y_) * CAP

    def one_round(r, act_ref, routes_ref, gates_ref, result_ref):
        started = []
        home = after if r == 0 else None
        box_r = box.at[r]
        back_r = back.at[r]

        def send(name, src, dst, peer, k=0, to=None):
            i = SEMS[name, k]
            copy = pltpu.make_async_remote_copy(
                src_ref=src, dst_ref=dst, send_sem=send_sem.at[i], recv_sem=recv_sem.at[r, i],
                device_id={"expert": peer} if to is None else {"section": to, "expert": peer}, device_id_type=MESH,
            )
            copy.start()
            started.append(copy)

        def arrived(name, dst, k=0):
            i = SEMS[name, k]
            pltpu.make_async_remote_copy(
                src_ref=dst, dst_ref=dst, send_sem=send_sem.at[i], recv_sem=recv_sem.at[r, i],
                device_id={"expert": mate}, device_id_type=MESH,
            ).wait_recv()

        def five(ref, h, start):
            return ref.at[pl.ds(0, 2) if h is None else h, pl.ds(start, CAP)]

        def place(h, c_, k, y_):
            return five(box_r, h, base(c_, k, y_))

        values = act_ref[...].astype(jnp.float32)
        scale = lax.rsqrt(jnp.mean(values * values, axis=-1, keepdims=True) + EPS)
        normed = (values * scale * gain_ref[...]).astype(jnp.bfloat16)
        if r == 0:
            pack_m[0] = packer(routes_ref[...].astype(jnp.float32))
        tall = jnp.concatenate([normed[:, f * width:(f + 1) * width] for f in range(FOLD)], axis=0)
        packed = dot(pack_m[r], tall).astype(jnp.bfloat16)
        for h in range(2):
            sent[h] = packed[:, h * half:(h + 1) * half].reshape(EXPERTS * CAP, FOLD, half)
        if r == 0:
            pl.semaphore_wait(barrier, 15)

        send("zf", five(sent, None, e2 * CAP), place(None, c, 2, y), far)
        send("zc", five(sent, None, e1 * CAP), place(None, c, 3, y), up)
        send("zd", five(sent, None, e3 * CAP), place(None, c, 1, y), down)

        def y_send(k):
            piece = place(None, c, k, y)
            src = piece if k else five(sent, None, e * CAP)
            send("yr", src, piece, right, k)
            send("yl", src, piece, left, k)
            send("ya", src, piece, across, k)
            send("m0", src, piece, mate, k)

        def y_near(k):
            arrived("yr", place(None, c, k, y3), k)
            send("m1", place(None, c, k, y3), place(None, c, k, y3), mate, k)
            arrived("yl", place(None, c, k, y1), k)
            send("m2", place(None, c, k, y1), place(None, c, k, y1), mate, k)

        def y_last(k):
            arrived("ya", place(None, c, k, y2), k)
            send("m3", place(None, c, k, y2), place(None, c, k, y2), mate, k)

        def gathered(k):
            for name, y_ in (("m0", y), ("m1", y3), ("m2", y1), ("m3", y2)):
                arrived(name, place(None, oc, k, y_), k)

        def experts(lo, hi):
            groups = range(lo // FOLD, hi // FOLD)
            swap = swap_m[...]
            for g in groups:
                block = jnp.concatenate(
                    [box[r, h, g * FOLD:(g + 1) * FOLD].reshape(FOLD * FOLD, half) for h in range(2)], axis=1
                )
                block = dot(swap, block).astype(jnp.bfloat16)
                for f in range(FOLD):
                    flat[g * FOLD:(g + 1) * FOLD, f * width:(f + 1) * width] = block[f * FOLD:(f + 1) * FOLD]
            both = dot(flat[lo:hi], wgu[...])
            gate_val, up_val = both[:, :hidden_units], both[:, hidden_units:]
            hidden = (gate_val / (1.0 + jnp.exp(-gate_val)) * up_val).astype(jnp.bfloat16)
            for f in range(FOLD):
                piece = dot(hidden, wd[:, f * width:(f + 1) * width]).astype(jnp.bfloat16)
                for g in groups:
                    stack[g, f * FOLD:(f + 1) * FOLD] = piece[g * FOLD - lo:(g + 1) * FOLD - lo]
            for g in groups:
                block = dot(swap, stack[g]).astype(jnp.bfloat16)
                for h in range(2):
                    parts[h, g * FOLD:(g + 1) * FOLD] = block[:, h * half:(h + 1) * half].reshape(FOLD, FOLD, half)

        wide = 4 * CAP

        def to_mate(k):
            send("c1", parts.at[:, pl.ds(base(oc, k, 0), wide)], core_in.at[r, k], mate, k)

        def sum_cores(k):
            arrived("c1", core_in.at[r, k], k)
            mine = parts[:, pl.ds(base(c, k, 0), wide)].astype(jnp.float32)
            chip_sum[k] = (mine + core_in[r, k].astype(jnp.float32)).astype(jnp.bfloat16)
            for name, y_, peer, at in (("sa", y2, across, 2), ("sr", y1, right, 0), ("sl", y3, left, 1)):
                send(name, chip_sum.at[k, :, pl.ds(y_ * CAP, CAP)], y_in.at[r, at, k], peer, k)

        def sum_all(k):
            total = chip_sum[k, :, pl.ds(y * CAP, CAP)].astype(jnp.float32)
            for at, name in enumerate(("sr", "sl", "sa")):
                arrived(name, y_in.at[r, at, k], k)
                total = total + y_in[r, at, k].astype(jnp.float32)
            if k == 0 and r == 1:
                back[r, :, pl.ds(e * CAP, CAP)] = total.astype(jnp.bfloat16)
            else:
                final[k] = total.astype(jnp.bfloat16)
            if k == 0 and r == 0:
                send("ro", final.at[0], five(back_r, None, e * CAP), me, 0, home)
            if k == 2:
                send("rf", final.at[2], five(back_r, None, e * CAP), far, 0, home)
            if k == 1:
                send("rc", final.at[1], five(back_r, None, e * CAP), up, 0, home)
            if k == 3:
                send("rd", final.at[3], five(back_r, None, e * CAP), down, 0, home)

        y_send(0)
        box[r, :, pl.ds(base(c, 0, y), CAP)] = sent[:, pl.ds(e * CAP, CAP)]
        if r == 0:
            swap_m[...] = transposer()
            pack_m[1] = packer(r2_ref[...].astype(jnp.float32))
            unpack_m[1] = unpacker(r2_ref[...].astype(jnp.float32))
            info[0:1, 0:rows] = routes_ref[...].astype(jnp.float32)
            info[1:2, 0:rows] = gates_ref[...]
            for q in range(2):
                for lo in (40, 168):
                    box[q, :, lo:lo + 8] = jnp.zeros((2, 8, FOLD, half), jnp.bfloat16)
            for load in loads:
                load.wait()
        y_near(0)
        y_last(0)
        gathered(0)
        experts(0, 48)
        to_mate(0)
        arrived("zc", place(None, c, 3, y))
        y_send(3)
        arrived("zd", place(None, c, 1, y))
        y_send(1)
        sum_cores(0)
        y_near(3)
        y_near(1)
        arrived("zf", place(None, c, 2, y))
        y_send(2)
        if r == 0:
            send("tok", act_ref, tokens_in, me, 0, after)
            send("inf", info, info_in, me, 0, after)
        y_last(3)
        y_last(1)
        sum_all(0)
        y_near(2)
        y_last(2)
        gathered(2)
        experts(128, 176)
        to_mate(2)
        gathered(1)
        gathered(3)
        experts(48, 128)
        to_mate(1)
        to_mate(3)
        sum_cores(2)
        sum_cores(1)
        sum_cores(3)
        sum_all(2)
        sum_all(1)
        sum_all(3)
        if r == 0:
            arrived("tok", tokens_in)
            arrived("inf", info_in)
            unpack_m[0] = unpacker(info_in[0:1, 0:rows])
        gate_column = column(info_in[1:2, 0:rows] if r == 0 else gates_ref[...])
        for copy in started:
            copy.wait_send()
        if r == 0:
            arrived("ro", five(back_r, None, e * CAP))
        arrived("rc", five(back_r, None, e3 * CAP))
        arrived("rd", five(back_r, None, e1 * CAP))
        arrived("rf", five(back_r, None, e2 * CAP))

        got = jnp.concatenate([back[r, h].reshape(EXPERTS * CAP * FOLD, half) for h in range(2)], axis=1)
        got = dot(unpack_m[r], got)
        got = jnp.concatenate([got[f * rows:(f + 1) * rows] for f in range(FOLD)], axis=1)
        base_ref = tokens_in if r == 0 else act_ref
        update = (gate_column * got).astype(jnp.bfloat16)
        result_ref[...] = (base_ref[...].astype(jnp.float32) + update.astype(jnp.float32)).astype(jnp.bfloat16)
    one_round(0, x_ref, r1_ref, g1_ref, carried)
    one_round(1, carried, r2_ref, g2_ref, out_ref)


def on_device(n_section, tokens, norm_gain, first_routes, first_gates, second_routes, second_gates, gate_proj, up_proj, down_proj):
    rows, depth = tokens.shape[1:]
    units = gate_proj.shape[-1]
    half = depth // FOLD // 2
    slots = SLOTS
    cells = FOLD * rows
    bf16 = jnp.bfloat16
    near = pl.BlockSpec(memory_space=pltpu.VMEM)
    far = pl.BlockSpec(memory_space=pl.ANY)
    return pl.pallas_call(
        functools.partial(kernel, n_section),
        out_shape=jax.ShapeDtypeStruct((rows, depth), bf16),
        in_specs=[near] * 6 + [far] * 3,
        out_specs=near,
        scratch_shapes=[
            pltpu.VMEM((depth, 2 * units), bf16),
            pltpu.VMEM((units, depth), bf16),
            pltpu.VMEM((2, EXPERTS * CAP, FOLD, half), bf16),
            pltpu.VMEM((2, 2, slots, FOLD, half), bf16),
            pltpu.VMEM((slots, depth), bf16),
            pltpu.VMEM((slots // FOLD, FOLD * FOLD, depth // FOLD), bf16),
            pltpu.VMEM((2, slots, FOLD, half), bf16),
            pltpu.VMEM((2, 4, 2, 4 * CAP, FOLD, half), bf16),
            pltpu.VMEM((4, 2, 4 * CAP, FOLD, half), bf16),
            pltpu.VMEM((2, 3, 4, 2, CAP, FOLD, half), bf16),
            pltpu.VMEM((4, 2, CAP, FOLD, half), bf16),
            pltpu.VMEM((2, 2, EXPERTS * CAP, FOLD, half), bf16),
            pltpu.VMEM((rows, depth), bf16),
            pltpu.VMEM((8, 128), jnp.float32),
            pltpu.VMEM((8, 128), jnp.float32),
            pltpu.VMEM((rows, depth), bf16),
            pltpu.VMEM((2, EXPERTS * CAP * FOLD, cells), bf16),
            pltpu.VMEM((2, cells, EXPERTS * CAP * FOLD), bf16),
            pltpu.VMEM((FOLD * FOLD, FOLD * FOLD), bf16),
            pltpu.SemaphoreType.DMA((3,)),
            pltpu.SemaphoreType.DMA((len(SEMS),)),
            pltpu.SemaphoreType.DMA((2, len(SEMS))),
        ],
        compiler_params=pltpu.CompilerParams(collective_id=0, has_side_effects=True),
    )(
        tokens[0], norm_gain, *(a.reshape(1, rows) for a in (first_routes, first_gates, second_routes, second_gates)),
        gate_proj[0, 0], up_proj[0, 0], down_proj[0, 0],
    )[None]


def solution(mesh):
    rows = P("section", "expert", None)
    weights = P("section", "expert", None, None)
    return jax.shard_map(
        functools.partial(on_device, mesh.shape["section"]),
        mesh=mesh,
        in_specs=(rows, P("section", None), rows, rows, rows, rows, weights, weights, weights),
        out_specs=rows,
        check_vma=False,
    )
```
